128 devices in a mesh: row: 8 (over y_hi, z), col: 16 (over y_lo, x, core).
Axes of the slice: x: 4, y: 4 (y_hi: 2, y_lo: 2; y = y_hi * 2 + y_lo), z: 4, core: 2. Of those that a mesh axis runs over, the one named last changes fastest.
Arguments:
- a_blocks: float32 [8, 16, 32, 128, 128], P('row', 'col'), may hold values from -1 to 1
- a_rows: int32 [8, 16, 32], P('row', 'col'), may hold values from 0 to 127, as said below
- a_cols: int32 [8, 16, 32], P('row', 'col'), may hold values from 0 to 15, as said below
- a_counts: int32 [8, 16, 16], P('row', 'col'), may hold values from 0 to 2, as said below
- b_blocks: float32 [8, 16, 32, 128, 128], P('row', 'col'), may hold values from -1 to 1
- b_rows: int32 [8, 16, 32], P('row', 'col'), may hold values from 0 to 15, as said below
- b_cols: int32 [8, 16, 32], P('row', 'col'), may hold values from 0 to 63, as said below
- b_counts: int32 [8, 16, 16], P('row', 'col'), may hold values from 0 to 2, as said below
- out_mask: int32 [128, 64], P('row', 'col'), may hold values 0 or 1
Outputs:
- square: float32 [16384, 8192], P('row', 'col')
The draws below stay inside these ranges and needn't reach their ends.
Inputs may be any that keep to these rules, and one draw needn't show every extreme that they name: a_counts[i, j, k] is the number of counted slots of device (i, j)'s list with inner block index k, at most 2; for every i and k some device (i, j) has exactly 2. The counted slots come first in the list, ordered by inner block index. `a_rows`: a device (i, j) lists only block rows from i * 16 to (i + 1) * 16 - 1; no block (r, k) is listed twice among counted slots. `a_cols`: on counted slots, the inner block index agrees with a_counts. b_counts[i, j, k] is the number of counted slots of device (i, j)'s list with inner block index k, at most 2; for every j and k some device (i, j) has exactly 2. The counted slots come first in the list, ordered by inner block index. `b_rows`: on counted slots, the inner block index agrees with b_counts. `b_cols`: a device (i, j) lists only block columns from j * 4 to (j + 1) * 4 - 1; no block (k, c) is listed twice among counted slots.
All inputs are finite; a program needn't handle non-finite values. No bound on the sum of `out_mask` on one device may be relied on, other than what follows from the above.
Results may differ from the reference program's by a relative error of at most 0.00007.
Values sent between devices are 32-bit elements; how exact they have to be, the bound alone decides.
No kernel may reach another device: no remote copies, remote signals or barrier semaphores. Data moves between devices by JAX's collectives and lax.ppermute only.
A program may use at most 64 MiB of HBM per device.

```python
import jax
import jax.numpy as jnp
from jax import lax

BS = 128
CAP = 2
RB = 16
CB = 4
KB = 16
MB = 128
NBC = 64
LIST = 32
N_ROW = 8
N_COL = 16


def block_lists(key, groups, members, inner_count, group_size):
    key_want, key_lead, key_order, key_inner, key_owner = jax.random.split(key, 5)
    wanted = jax.random.randint(key_want, (groups, members, inner_count), 0, CAP + 1)
    leader = jax.random.randint(key_lead, (groups, inner_count), 0, members)
    member_ids = jnp.arange(members, dtype=jnp.int32)
    wanted = jnp.where(member_ids[None, :, None] == leader[:, None, :], CAP, wanted)
    rank_order = (member_ids[None, :, None] - leader[:, None, :]) % members
    earlier = rank_order[:, None, :, :] < rank_order[:, :, None, :]
    preceding = jnp.sum(jnp.where(earlier, wanted[:, None, :, :], 0), axis=2).astype(jnp.int32)
    counts = jnp.clip(group_size - preceding, 0, wanted).astype(jnp.int32)
    scores = jax.random.randint(key_order, (groups, inner_count, group_size), 0, 1 << 20) * group_size
    scores = scores + jnp.arange(group_size, dtype=jnp.int32)[None, None, :]
    shuffled = jnp.argsort(scores, axis=-1).astype(jnp.int32)
    starts = jnp.cumsum(counts, axis=-1) - counts
    finish = starts + counts
    slot_index = jnp.arange(LIST, dtype=jnp.int32)
    inner_of = jnp.sum((finish[:, :, :, None] <= slot_index[None, None, None, :]).astype(jnp.int32), axis=2)
    inner_safe = jnp.minimum(inner_of, inner_count - 1).astype(jnp.int32)
    group_ids = jnp.arange(groups, dtype=jnp.int32)[:, None, None]
    member_grid = member_ids[None, :, None]
    start_of = starts[group_ids, member_grid, inner_safe]
    before_of = preceding[group_ids, member_grid, inner_safe]
    position = jnp.clip(slot_index[None, None, :] - start_of + before_of, 0, group_size - 1)
    picked = shuffled[group_ids, inner_safe, position]
    usable = slot_index[None, None, :] < jnp.sum(counts, axis=-1)[:, :, None]
    filler_inner = jax.random.randint(key_inner, (groups, members, LIST), 0, inner_count)
    filler_owner = jax.random.randint(key_owner, (groups, members, LIST), 0, groups * group_size)
    inner_index = jnp.where(usable, inner_safe, filler_inner).astype(jnp.int32)
    owner_index = jnp.where(usable, group_ids * group_size + picked, filler_owner).astype(jnp.int32)
    return (inner_index, owner_index, counts)


def lists_rows(key):
    return block_lists(jax.random.fold_in(key, 11), N_ROW, N_COL, KB, RB)


def lists_cols(key):
    inner_index, owner_index, counts = block_lists(jax.random.fold_in(key, 23), N_COL, N_ROW, KB, CB)
    return (jnp.transpose(inner_index, (1, 0, 2)), jnp.transpose(owner_index, (1, 0, 2)), jnp.transpose(counts, (1, 0, 2)))


def draw_a_rows(key, part):
    return lists_rows(key)[1]


def draw_a_cols(key, part):
    return lists_rows(key)[0]


def draw_a_counts(key, part):
    return lists_rows(key)[2]


def draw_b_rows(key, part):
    return lists_cols(key)[0]


def draw_b_cols(key, part):
    return lists_cols(key)[1]


def draw_b_counts(key, part):
    return lists_cols(key)[2]


def touch_ends(result, own_key, smallest, top_value):
    extent = result.shape
    index_at = [jax.random.randint(jax.random.fold_in(own_key, axis), (), 0, extent[axis]) for axis in range(len(extent))]
    result = result.at[tuple(index_at)].set(smallest)
    longest = extent.index(max(extent))
    index_at[longest] = (index_at[longest] + 1) % extent[longest]
    return result.at[tuple(index_at)].set(top_value)


def block_levels(rng, dims, cuts, low, largest):
    factor_of, own = 1.0, jax.random.fold_in(rng, 6)
    for axis_at, shards_of in cuts:
        steps = jnp.exp(jax.random.uniform(jax.random.fold_in(own, axis_at), (shards_of,), jnp.float32, low / len(cuts), largest / len(cuts)))
        factor_of = factor_of * jnp.repeat(steps, dims[axis_at] // shards_of).reshape([-1 if axis == axis_at else 1 for axis in range(len(dims))])
    return factor_of


def centred(stream_key, extent, deviation, limit, cuts=(), held_as=jnp.bfloat16):
    entries = deviation * jax.random.normal(stream_key, extent, jnp.float32)
    if cuts:
        entries = entries * block_levels(stream_key, extent, cuts, -0.22, 0.18)
    return jnp.clip(entries, -limit, limit).astype(held_as)


def setup_inputs(seed: int = 0) -> dict:
    arg_keys = jax.random.split(jax.random.key(seed), 10)
    a_blocks = centred(arg_keys[0], (N_ROW, N_COL, LIST, BS, BS), 0.18, 1.0, ((0, 8), (1, 16)), jnp.float32)
    a_rows = draw_a_rows(jax.random.fold_in(arg_keys[9], 71), 0)
    a_cols = draw_a_cols(jax.random.fold_in(arg_keys[9], 71), 0)
    a_counts = draw_a_counts(jax.random.fold_in(arg_keys[9], 71), 0)
    b_blocks = centred(arg_keys[4], (N_ROW, N_COL, LIST, BS, BS), 0.18, 1.0, ((0, 8), (1, 16)), jnp.float32)
    b_rows = draw_b_rows(jax.random.fold_in(arg_keys[9], 71), 0)
    b_cols = draw_b_cols(jax.random.fold_in(arg_keys[9], 71), 0)
    b_counts = draw_b_counts(jax.random.fold_in(arg_keys[9], 71), 0)
    out_mask = touch_ends((jax.random.randint(arg_keys[8], (MB, NBC), 0, 4) < 3).astype(jnp.int32), jax.random.fold_in(arg_keys[8], 1), 0, 1)
    return {"a_blocks": a_blocks, "a_rows": a_rows, "a_cols": a_cols, "a_counts": a_counts, "b_blocks": b_blocks, "b_rows": b_rows, "b_cols": b_cols, "b_counts": b_counts, "out_mask": out_mask}


def dense_from(blocks, outer, inner, counts, n_first, n_second):
    block_width = blocks.shape[-1]
    totals = jnp.sum(counts, axis=-1)
    slot_index = jnp.arange(blocks.shape[2], dtype=jnp.int32)
    usable = slot_index[None, None, :] < totals[:, :, None]
    flat = (outer * n_second + inner).astype(jnp.int32)
    flat = jnp.where(usable, flat, n_first * n_second)
    dense = jnp.zeros((n_first * n_second, block_width, block_width), jnp.float32)
    dense = dense.at[flat.reshape(-1)].add(blocks.reshape((-1, block_width, block_width)), mode="drop")
    dense = dense.reshape((n_first, n_second, block_width, block_width)).transpose((0, 2, 1, 3))
    return dense.reshape((n_first * block_width, n_second * block_width))


def reference(a_blocks, a_rows, a_cols, a_counts, b_blocks, b_rows, b_cols, b_counts, out_mask):
    slab_rows = dense_from(a_blocks, a_rows, a_cols, a_counts, MB, KB)
    slab_cols = dense_from(b_blocks, b_rows, b_cols, b_counts, KB, NBC)
    product = jnp.dot(slab_rows, slab_cols, precision=lax.Precision.HIGHEST, preferred_element_type=jnp.float32)
    shaped = product.reshape((MB, BS, NBC, BS)) * out_mask.astype(jnp.float32)[:, None, :, None]
    return shaped.reshape((MB * BS, NBC * BS))
```

```python
import functools

import jax
import jax.numpy as jnp
from jax import lax
from jax.experimental import pallas as pl
from jax.experimental.pallas import tpu as pltpu
from jax.sharding import PartitionSpec as P

BS = 128
CAP = 2
NX, NY, NC, NZ = 4, 2, 2, 4
N_COL = NY * NX * NC
N_ROW = 2 * NZ
KB = 16
KZ = KB // NZ
RB = 16
CB = 4
MET = 8
F32 = jnp.float32
ANY = pl.BlockSpec(memory_space=pl.ANY)
SMEM = pl.BlockSpec(memory_space=pltpu.SMEM)
VMEM = pl.BlockSpec(memory_space=pltpu.VMEM)


def col_id(y, x, c):
    return (y % NY) * NX * NC + (x % NX) * NC + c % NC


def col_shift(value, dy=0, dx=0, dc=0):
    route = [
        (col_id(y, x, c), col_id(y + dy, x + dx, c + dc))
        for y in range(NY)
        for x in range(NX)
        for c in range(NC)
    ]
    return lax.ppermute(value, "col", route)


def row_shift(value, dy=0, dz=0):
    route = [
        (y * NZ + z, (y + dy) % 2 * NZ + (z + dz) % NZ) for y in range(2) for z in range(NZ)
    ]
    return lax.ppermute(value, "row", route)


def lane_marks(first, second):
    lane = lax.broadcasted_iota(jnp.int32, (MET, BS), 1)
    marks = jnp.where(lane == 0, first, jnp.where(lane == 1, second, -1))
    return marks.astype(F32)


def pack_a_kernel(counts, owners, blocks, send, marks, sems, mark_sem):
    start = jnp.int32(0)
    jobs = []
    for k in range(KB):
        count = counts[k]
        places = []
        for rank in range(CAP):
            slot = jnp.minimum(start + rank, blocks.shape[0] - 1)
            copy = pltpu.make_async_copy(
                blocks.at[slot], send.at[k, pl.ds(rank * BS, BS)], sems.at[k, rank]
            )
            have = count > rank
            pl.when(have)(copy.start)
            jobs.append((have, copy))
            places.append(jnp.where(have, lax.rem(owners[slot], RB), -1))
        marks[k] = lane_marks(*places)
        start = start + count
    tail = pltpu.make_async_copy(marks, send.at[:, pl.ds(CAP * BS, MET)], mark_sem)
    tail.start()
    for have, copy in jobs:
        pl.when(have)(copy.wait)
    tail.wait()


def pack_a(counts, owners, blocks):
    return pl.pallas_call(
        pack_a_kernel,
        out_shape=jax.ShapeDtypeStruct((N_COL, CAP * BS + MET, BS), F32),
        in_specs=[SMEM, SMEM, ANY],
        out_specs=ANY,
        scratch_shapes=[
            pltpu.VMEM((KB, MET, BS), F32),
            pltpu.SemaphoreType.DMA((KB, CAP)),
            pltpu.SemaphoreType.DMA,
        ],
        name="pack_a",
    )(counts, owners, blocks)


def pack_b_kernel(z_ref, counts, owners, blocks, *rest):
    sends, (marks, starts, sems, mark_sem) = rest[:NZ], rest[NZ:]
    start = jnp.int32(0)
    for k in range(KB):
        starts[k] = start
        start = start + counts[k]
    jobs = []
    tails = []
    for rel in range(NZ):
        base = lax.rem(z_ref[0] + rel, NZ) * KZ
        for kk in range(KZ):
            count = counts[base + kk]
            places = []
            for rank in range(CAP):
                slot = jnp.minimum(starts[base + kk] + rank, blocks.shape[0] - 1)
                piece = kk * CAP + rank
                copy = pltpu.make_async_copy(
                    blocks.at[slot], sends[rel].at[pl.ds(piece * BS, BS)], sems.at[rel, piece]
                )
                have = count > rank
                pl.when(have)(copy.start)
                jobs.append((have, copy))
                places.append(jnp.where(have, lax.rem(owners[slot], CB), -1))
            marks[rel, pl.ds(kk * MET, MET)] = lane_marks(*places)
        tail = pltpu.make_async_copy(
            marks.at[rel], sends[rel].at[pl.ds(KZ * CAP * BS, KZ * MET)], mark_sem.at[rel]
        )
        tail.start()
        tails.append(tail)
    for have, copy in jobs:
        pl.when(have)(copy.wait)
    for tail in tails:
        tail.wait()


def pack_b(z_now, counts, owners, blocks):
    rows = KZ * (CAP * BS + MET)
    return pl.pallas_call(
        pack_b_kernel,
        out_shape=[jax.ShapeDtypeStruct((rows, BS), F32)] * NZ,
        in_specs=[SMEM, SMEM, SMEM, ANY],
        out_specs=[ANY] * NZ,
        scratch_shapes=[
            pltpu.VMEM((NZ, KZ * MET, BS), F32),
            pltpu.SMEM((KB,), jnp.int32),
            pltpu.SemaphoreType.DMA((NZ, KZ * CAP)),
            pltpu.SemaphoreType.DMA((NZ,)),
        ],
        name="pack_b",
    )(z_now, counts, owners, blocks)


def unpack_a_kernel(got, panel, marks, sems, mark_sem):
    read = pltpu.make_async_copy(got.at[:, CAP * BS], marks, mark_sem)
    read.start()
    panel[...] = jnp.zeros_like(panel)
    read.wait()
    jobs = []
    for source in range(N_COL):
        for rank in range(CAP):
            place = marks[source, rank].astype(jnp.int32)
            have = place >= 0
            at = pl.multiple_of(jnp.maximum(place, 0) * BS, BS)
            copy = pltpu.make_async_copy(
                got.at[source, pl.ds(rank * BS, BS)], panel.at[pl.ds(at, BS)], sems.at[source, rank]
            )
            pl.when(have)(copy.start)
            jobs.append((have, copy))
    for have, copy in jobs:
        pl.when(have)(copy.wait)


def unpack_a(got):
    return pl.pallas_call(
        unpack_a_kernel,
        out_shape=jax.ShapeDtypeStruct((RB * BS, BS), F32),
        in_specs=[ANY],
        out_specs=VMEM,
        scratch_shapes=[
            pltpu.SMEM((N_COL, BS), F32),
            pltpu.SemaphoreType.DMA((N_COL, CAP)),
            pltpu.SemaphoreType.DMA,
        ],
        name="unpack_a",
    )(got)


def unpack_b_kernel(*refs):
    gots, (panel, marks, sems, mark_sem) = refs[:NZ], refs[NZ:]
    reads = []
    for rel in range(NZ):
        read = pltpu.make_async_copy(
            gots[rel].at[pl.ds(KZ * CAP * BS, KZ * MET)], marks.at[rel], mark_sem.at[rel]
        )
        read.start()
        reads.append(read)
    panel[...] = jnp.zeros_like(panel)
    for read in reads:
        read.wait()
    jobs = []
    for rel in range(NZ):
        for kk in range(KZ):
            for rank in range(CAP):
                place = marks[rel, kk * MET, rank].astype(jnp.int32)
                have = place >= 0
                at = pl.multiple_of(jnp.maximum(place, 0) * BS, BS)
                piece = kk * CAP + rank
                copy = pltpu.make_async_copy(
                    gots[rel].at[pl.ds(piece * BS, BS)],
                    panel.at[pl.ds(kk * BS, BS), pl.ds(at, BS)],
                    sems.at[rel, piece],
                )
                pl.when(have)(copy.start)
                jobs.append((have, copy))
    for have, copy in jobs:
        pl.when(have)(copy.wait)


def unpack_b(gots):
    return pl.pallas_call(
        unpack_b_kernel,
        out_shape=jax.ShapeDtypeStruct((KZ * BS, CB * BS), F32),
        in_specs=[ANY] * NZ,
        out_specs=VMEM,
        scratch_shapes=[
            pltpu.SMEM((NZ, KZ * MET, BS), F32),
            pltpu.SemaphoreType.DMA((NZ, KZ * CAP)),
            pltpu.SemaphoreType.DMA((NZ,)),
        ],
        name="unpack_b",
    )(*gots)


PHASES = (8, 6, 2)


def split(value):
    high = value.astype(jnp.bfloat16)
    return high, (value - high.astype(F32)).astype(jnp.bfloat16)


def order_b_kernel(order, here, ahead, behind, far_lo, far_hi, *rest):
    outs, (panel, sems) = rest[:6], rest[6:]
    half = KZ // 2
    z_now = order[KB]
    jobs = []
    for p in range(KB):
        k = order[p]
        rel = lax.rem(k // KZ - z_now + NZ, NZ)
        kk = lax.rem(k, KZ)
        row = pl.multiple_of(kk * BS, BS)
        row_hi = pl.multiple_of(jnp.maximum(kk - half, 0) * BS, BS)
        row_lo = pl.multiple_of(jnp.minimum(kk, half - 1) * BS, BS)
        for want, source in (
            (rel == 0, here.at[pl.ds(row, BS)]),
            (rel == 1, ahead.at[pl.ds(row, BS)]),
            (rel == 3, behind.at[pl.ds(row, BS)]),
            ((rel == 2) & (kk < half), far_lo.at[pl.ds(row_lo, BS)]),
            ((rel == 2) & (kk >= half), far_hi.at[pl.ds(row_hi, BS)]),
        ):
            copy = pltpu.make_async_copy(source, panel.at[pl.ds(p * BS, BS)], sems.at[p])
            pl.when(want)(copy.start)
        jobs.append(pltpu.make_async_copy(here.at[pl.ds(0, BS)], panel.at[pl.ds(p * BS, BS)], sems.at[p]))
    p = 0
    for i, n in enumerate(PHASES):
        for q in range(n):
            jobs[p].wait()
            high, low = split(panel[pl.ds(p * BS, BS), :])
            outs[2 * i][pl.ds(q * BS, BS), :] = high
            outs[2 * i + 1][pl.ds(q * BS, BS), :] = low
            p += 1


def order_b(order, pieces):
    outs = [
        jax.ShapeDtypeStruct((n * BS, CB * BS), jnp.bfloat16) for n in PHASES for _ in range(2)
    ]
    return pl.pallas_call(
        order_b_kernel,
        out_shape=outs,
        in_specs=[SMEM] + [ANY] * 5,
        out_specs=[VMEM] * 6,
        scratch_shapes=[
            pltpu.VMEM((KB * BS, CB * BS), F32),
            pltpu.SemaphoreType.DMA((KB,)),
        ],
        name="order_b",
    )(order, *pieces)


TM = 256


def product_kernel(n_whole, n_half, first, last, *refs):
    refs = list(refs)
    mask = refs.pop(0) if last else None
    whole = [refs.pop(0) for _ in range(n_whole)]
    halves = [(refs.pop(0), refs.pop(0)) for _ in range(n_half)]
    b_high, b_low = refs.pop(0), refs.pop(0)
    before = None if first else refs.pop(0)
    out = refs.pop(0)
    tile = pl.program_id(0)
    upper = tile < pl.num_programs(0) // 2
    columns = [ref[...] for ref in whole]
    columns += [jnp.where(upper, lo[...], hi[...]) for lo, hi in halves]
    high, low = split(jnp.concatenate(columns, axis=1))
    total = jnp.dot(high, b_high[...], preferred_element_type=F32)
    total += jnp.dot(high, b_low[...], preferred_element_type=F32)
    total += jnp.dot(low, b_high[...], preferred_element_type=F32)
    if not first:
        total += before[...]
    if last:
        for r in range(TM // BS):
            for c in range(CB):
                keep = mask[tile * (TM // BS) + r, c].astype(F32)
                piece = total[r * BS : (r + 1) * BS, c * BS : (c + 1) * BS]
                out[pl.ds(r * BS, BS), pl.ds(c * BS, BS)] = piece * keep
    else:
        out[...] = total


def product(whole, halves, b_pair, before=None, mask=None):
    rows, cols = RB * BS, CB * BS
    tiles = rows // TM
    depth = b_pair[0].shape[0]
    a_spec = pl.BlockSpec((TM, BS), lambda t: (t, 0))
    lo_spec = pl.BlockSpec((TM, BS), lambda t: (jnp.minimum(t, tiles // 2 - 1), 0))
    hi_spec = pl.BlockSpec((TM, BS), lambda t: (jnp.maximum(t - tiles // 2, 0), 0))
    b_spec = pl.BlockSpec((depth, cols), lambda t: (0, 0))
    c_spec = pl.BlockSpec((TM, cols), lambda t: (t, 0))
    args, specs = [], []
    if mask is not None:
        args.append(mask)
        specs.append(SMEM)
    args += whole
    specs += [a_spec] * len(whole)
    for pair in halves:
        args += pair
        specs += [lo_spec, hi_spec]
    args += b_pair
    specs += [b_spec] * 2
    if before is not None:
        args.append(before)
        specs.append(c_spec)
    return pl.pallas_call(
        functools.partial(
            product_kernel, len(whole), len(halves), before is None, mask is not None
        ),
        grid=(tiles,),
        out_shape=jax.ShapeDtypeStruct((rows, cols), F32),
        in_specs=specs,
        out_specs=c_spec,
        cost_estimate=pl.CostEstimate(
            flops=6 * rows * cols * depth,
            bytes_accessed=4 * (rows * depth + depth * cols + 2 * rows * cols),
            transcendentals=0,
        ),
        name="product",
    )(*args)


def per_device(a_blocks, a_rows, a_cols, a_counts, b_blocks, b_rows, b_cols, b_counts, out_mask):
    row_now = lax.axis_index("row")
    col_now = lax.axis_index("col")
    z_now = row_now % NZ
    y_now, x_now, c_now = col_now // (NX * NC), col_now // NC % NX, col_now % NC

    b_send = pack_b(
        z_now.reshape(1), b_counts.reshape(-1), b_cols.reshape(-1), b_blocks.reshape(-1, BS, BS)
    )
    a_send = pack_a(a_counts.reshape(-1), a_rows.reshape(-1), a_blocks.reshape(-1, BS, BS))
    b_got = [b_send[0]] + [row_shift(b_send[rel], dz=rel) for rel in range(1, NZ)]
    a_got = lax.all_to_all(a_send, "col", split_axis=0, concat_axis=0, tiled=True)

    b_part = unpack_b(b_got)
    b_here = b_part + row_shift(b_part, dy=1)
    half = KZ * BS // 2
    b_behind = row_shift(b_here, dz=1)
    b_ahead = row_shift(b_here, dz=-1)
    b_far_lo = row_shift(b_behind[:half], dz=1)
    b_far_hi = row_shift(b_ahead[half:], dz=-1)

    def swap(value):
        return col_shift(value, dc=1)

    half = RB * BS // 2
    plane = []
    own = unpack_a(a_got)
    other = col_shift(own, dy=1)
    for first in (own, other):
        behind = col_shift(first, dx=1)
        ahead = col_shift(first, dx=-1)
        far_lo = col_shift(behind[:half], dx=1)
        far_hi = col_shift(ahead[half:], dx=-1)
        plane.append((first, behind, ahead, far_lo, far_hi))

    def pairs(values):
        return [v for value in values for v in (value, swap(value))]

    def far_pairs(lo, hi):
        return [(lo, hi), (swap(lo), swap(hi))]

    def k_of(dy, dx):
        return [col_id(y_now + dy, x_now + dx, c_now + dc) for dc in (0, 1)]

    near = (0, -1, 1)
    order = [k for dx in near for k in k_of(0, dx)] + k_of(0, 2)
    order += [k for dx in near for k in k_of(1, dx)] + k_of(1, 2)
    order = jnp.stack(order + [z_now]).astype(jnp.int32)
    b_all = order_b(order, (b_here, b_ahead, b_behind, b_far_lo, b_far_hi))

    total = product(pairs(plane[0][:3]), far_pairs(*plane[0][3:]), b_all[0:2])
    total = product(pairs(plane[1][:3]), [], b_all[2:4], before=total)
    return product([], far_pairs(*plane[1][3:]), b_all[4:6], before=total, mask=out_mask)


def solution(mesh):
    lists = P("row", "col", None)
    blocks = P("row", "col", None, None, None)
    in_specs = (blocks, lists, lists, lists, blocks, lists, lists, lists, P("row", "col"))
    return jax.shard_map(
        per_device, mesh=mesh, in_specs=in_specs, out_specs=P("row", "col"), check_vma=False
    )
```

```python
import functools

import jax
import jax.numpy as jnp
from jax import lax
from jax.experimental import pallas as pl
from jax.experimental.pallas import tpu as pltpu
from jax.sharding import PartitionSpec as P

BS = 128
CAP = 2
NX, NY, NC, NZ = 4, 2, 2, 4
N_COL = NY * NX * NC
N_ROW = 2 * NZ
KB = 16
KZ = KB // NZ
RB = 16
CB = 4
MET = 8
F32 = jnp.float32
ANY = pl.BlockSpec(memory_space=pl.ANY)
SMEM = pl.BlockSpec(memory_space=pltpu.SMEM)
VMEM = pl.BlockSpec(memory_space=pltpu.VMEM)


def col_id(y, x, c):
    return (y % NY) * NX * NC + (x % NX) * NC + c % NC


def col_shift(value, dy=0, dx=0, dc=0):
    route = [
        (col_id(y, x, c), col_id(y + dy, x + dx, c + dc))
        for y in range(NY)
        for x in range(NX)
        for c in range(NC)
    ]
    return lax.ppermute(value, "col", route)


def row_shift(value, dy=0, dz=0):
    route = [
        (y * NZ + z, (y + dy) % 2 * NZ + (z + dz) % NZ) for y in range(2) for z in range(NZ)
    ]
    return lax.ppermute(value, "row", route)


def lane_marks(first, second):
    lane = lax.broadcasted_iota(jnp.int32, (MET, BS), 1)
    marks = jnp.where(lane == 0, first, jnp.where(lane == 1, second, -1))
    return marks.astype(F32)


def pack_a_kernel(counts, owners, blocks, send, sems):
    start = jnp.int32(0)
    jobs = []
    for k in range(KB):
        count = counts[k]
        places = []
        for rank in range(CAP):
            slot = jnp.minimum(start + rank, blocks.shape[0] - 1)
            copy = pltpu.make_async_copy(
                blocks.at[slot], send.at[k, pl.ds(rank * BS, BS)], sems.at[k, rank]
            )
            have = count > rank
            pl.when(have)(copy.start)
            jobs.append((have, copy))
            places.append(jnp.where(have, lax.rem(owners[slot], RB), -1))
        send[k, pl.ds(CAP * BS, MET)] = lane_marks(*places)
        start = start + count
    for have, copy in jobs:
        pl.when(have)(copy.wait)


def pack_a(counts, owners, blocks):
    return pl.pallas_call(
        pack_a_kernel,
        out_shape=jax.ShapeDtypeStruct((N_COL, CAP * BS + MET, BS), F32),
        in_specs=[SMEM, SMEM, ANY],
        out_specs=VMEM,
        scratch_shapes=[pltpu.SemaphoreType.DMA((KB, CAP))],
        name="pack_a",
    )(counts, owners, blocks)


def pack_b_kernel(z_ref, counts, owners, blocks, *rest):
    sends, (starts, sems) = rest[:NZ], rest[NZ:]
    start = jnp.int32(0)
    for k in range(KB):
        starts[k] = start
        start = start + counts[k]
    jobs = []
    for rel in range(NZ):
        base = lax.rem(z_ref[0] + rel, NZ) * KZ
        for kk in range(KZ):
            count = counts[base + kk]
            places = []
            for rank in range(CAP):
                slot = jnp.minimum(starts[base + kk] + rank, blocks.shape[0] - 1)
                piece = kk * CAP + rank
                copy = pltpu.make_async_copy(
                    blocks.at[slot], sends[rel].at[pl.ds(piece * BS, BS)], sems.at[rel, piece]
                )
                have = count > rank
                pl.when(have)(copy.start)
                jobs.append((have, copy))
                places.append(jnp.where(have, lax.rem(owners[slot], CB), -1))
            sends[rel][pl.ds(KZ * CAP * BS + kk * MET, MET)] = lane_marks(*places)
    for have, copy in jobs:
        pl.when(have)(copy.wait)


def pack_b(z_now, counts, owners, blocks):
    rows = KZ * (CAP * BS + MET)
    return pl.pallas_call(
        pack_b_kernel,
        out_shape=[jax.ShapeDtypeStruct((rows, BS), F32)] * NZ,
        in_specs=[SMEM, SMEM, SMEM, ANY],
        out_specs=[VMEM] * NZ,
        scratch_shapes=[
            pltpu.SMEM((KB,), jnp.int32),
            pltpu.SemaphoreType.DMA((NZ, KZ * CAP)),
        ],
        name="pack_b",
    )(z_now, counts, owners, blocks)


def unpack_a_kernel(got, panel, marks, sems, mark_sem):
    read = pltpu.make_async_copy(got.at[:, CAP * BS], marks, mark_sem)
    read.start()
    panel[...] = jnp.zeros_like(panel)
    read.wait()
    jobs = []
    for source in range(N_COL):
        for rank in range(CAP):
            place = marks[source, rank].astype(jnp.int32)
            have = place >= 0
            at = pl.multiple_of(jnp.maximum(place, 0) * BS, BS)
            copy = pltpu.make_async_copy(
                got.at[source, pl.ds(rank * BS, BS)], panel.at[pl.ds(at, BS)], sems.at[source, rank]
            )
            pl.when(have)(copy.start)
            jobs.append((have, copy))
    for have, copy in jobs:
        pl.when(have)(copy.wait)


def unpack_a(got):
    return pl.pallas_call(
        unpack_a_kernel,
        out_shape=jax.ShapeDtypeStruct((RB * BS, BS), F32),
        in_specs=[VMEM],
        out_specs=VMEM,
        scratch_shapes=[
            pltpu.SMEM((N_COL, BS), F32),
            pltpu.SemaphoreType.DMA((N_COL, CAP)),
            pltpu.SemaphoreType.DMA,
        ],
        name="unpack_a",
    )(got)


def unpack_b_kernel(*refs):
    gots, (panel, marks, sems, mark_sem) = refs[:NZ], refs[NZ:]
    reads = []
    for rel in range(NZ):
        read = pltpu.make_async_copy(
            gots[rel].at[pl.ds(KZ * CAP * BS, KZ * MET)], marks.at[rel], mark_sem.at[rel]
        )
        read.start()
        reads.append(read)
    panel[...] = jnp.zeros_like(panel)
    for read in reads:
        read.wait()
    jobs = []
    for rel in range(NZ):
        for kk in range(KZ):
            for rank in range(CAP):
                place = marks[rel, kk * MET, rank].astype(jnp.int32)
                have = place >= 0
                at = pl.multiple_of(jnp.maximum(place, 0) * BS, BS)
                piece = kk * CAP + rank
                copy = pltpu.make_async_copy(
                    gots[rel].at[pl.ds(piece * BS, BS)],
                    panel.at[pl.ds(kk * BS, BS), pl.ds(at, BS)],
                    sems.at[rel, piece],
                )
                pl.when(have)(copy.start)
                jobs.append((have, copy))
    for have, copy in jobs:
        pl.when(have)(copy.wait)


def unpack_b(gots):
    return pl.pallas_call(
        unpack_b_kernel,
        out_shape=jax.ShapeDtypeStruct((KZ * BS, CB * BS), F32),
        in_specs=[VMEM] * NZ,
        out_specs=VMEM,
        scratch_shapes=[
            pltpu.SMEM((NZ, KZ * MET, BS), F32),
            pltpu.SemaphoreType.DMA((NZ, KZ * CAP)),
            pltpu.SemaphoreType.DMA((NZ,)),
        ],
        name="unpack_b",
    )(*gots)


PHASES = (8, 6, 2)


def split(value):
    high = value.astype(jnp.bfloat16)
    return high, (value - high.astype(F32)).astype(jnp.bfloat16)


def order_b_kernel(order, here, ahead, behind, far_lo, far_hi, *rest):
    outs, (panel, sems) = rest[:3], rest[3:]
    half = KZ // 2
    z_now = order[KB]
    jobs = []
    for p in range(KB):
        k = order[p]
        rel = lax.rem(k // KZ - z_now + NZ, NZ)
        kk = lax.rem(k, KZ)
        row = pl.multiple_of(kk * BS, BS)
        row_hi = pl.multiple_of(jnp.maximum(kk - half, 0) * BS, BS)
        row_lo = pl.multiple_of(jnp.minimum(kk, half - 1) * BS, BS)
        for want, source in (
            (rel == 0, here.at[pl.ds(row, BS)]),
            (rel == 1, ahead.at[pl.ds(row, BS)]),
            (rel == 3, behind.at[pl.ds(row, BS)]),
            ((rel == 2) & (kk < half), far_lo.at[pl.ds(row_lo, BS)]),
            ((rel == 2) & (kk >= half), far_hi.at[pl.ds(row_hi, BS)]),
        ):
            copy = pltpu.make_async_copy(source, panel.at[pl.ds(p * BS, BS)], sems.at[p])
            pl.when(want)(copy.start)
        jobs.append(pltpu.make_async_copy(here.at[pl.ds(0, BS)], panel.at[pl.ds(p * BS, BS)], sems.at[p]))
    p = 0
    for i, n in enumerate(PHASES):
        for q in range(n):
            jobs[p].wait()
            high, low = split(panel[pl.ds(p * BS, BS), :])
            outs[i][pl.ds(q * BS, BS), :] = high
            outs[i][pl.ds((n + q) * BS, BS), :] = low
            outs[i][pl.ds((2 * n + q) * BS, BS), :] = high
            p += 1


def order_b(order, pieces):
    outs = [jax.ShapeDtypeStruct((3 * n * BS, CB * BS), jnp.bfloat16) for n in PHASES]
    return pl.pallas_call(
        order_b_kernel,
        out_shape=outs,
        in_specs=[SMEM] + [ANY] * 5,
        out_specs=[VMEM] * 3,
        scratch_shapes=[
            pltpu.VMEM((KB * BS, CB * BS), F32),
            pltpu.SemaphoreType.DMA((KB,)),
        ],
        name="order_b",
    )(order, *pieces)


TM = 512


def product_kernel(n_whole, n_half, first, last, *refs):
    refs = list(refs)
    mask = refs.pop(0) if last else None
    whole = [refs.pop(0) for _ in range(n_whole)]
    halves = [(refs.pop(0), refs.pop(0)) for _ in range(n_half)]
    b_stack = refs.pop(0)
    before = None if first else refs.pop(0)
    out = refs.pop(0)
    tile = pl.program_id(0)
    upper = tile < pl.num_programs(0) // 2
    columns = [ref[...] for ref in whole]
    columns += [jnp.where(upper, lo[...], hi[...]) for lo, hi in halves]
    high, low = split(jnp.concatenate(columns, axis=1))
    total = jnp.dot(
        jnp.concatenate([high, high, low], axis=1), b_stack[...], preferred_element_type=F32
    )
    if not first:
        total += before[...]
    if last:
        for r in range(TM // BS):
            for c in range(CB):
                keep = mask[tile * (TM // BS) + r, c].astype(F32)
                piece = total[r * BS : (r + 1) * BS, c * BS : (c + 1) * BS]
                out[pl.ds(r * BS, BS), pl.ds(c * BS, BS)] = piece * keep
    else:
        out[...] = total


def product(whole, halves, b_stack, before=None, mask=None):
    rows, cols = RB * BS, CB * BS
    tiles = rows // TM
    depth = b_stack.shape[0] // 3
    a_spec = pl.BlockSpec((TM, BS), lambda t: (t, 0))
    lo_spec = pl.BlockSpec((TM, BS), lambda t: (jnp.minimum(t, tiles // 2 - 1), 0))
    hi_spec = pl.BlockSpec((TM, BS), lambda t: (jnp.maximum(t - tiles // 2, 0), 0))
    b_spec = pl.BlockSpec((3 * depth, cols), lambda t: (0, 0))
    c_spec = pl.BlockSpec((TM, cols), lambda t: (t, 0))
    args, specs = [], []
    if mask is not None:
        args.append(mask)
        specs.append(SMEM)
    args += whole
    specs += [a_spec] * len(whole)
    for pair in halves:
        args += pair
        specs += [lo_spec, hi_spec]
    args.append(b_stack)
    specs.append(b_spec)
    if before is not None:
        args.append(before)
        specs.append(c_spec)
    return pl.pallas_call(
        functools.partial(
            product_kernel, len(whole), len(halves), before is None, mask is not None
        ),
        grid=(tiles,),
        out_shape=jax.ShapeDtypeStruct((rows, cols), F32),
        in_specs=specs,
        out_specs=c_spec,
        cost_estimate=pl.CostEstimate(
            flops=6 * rows * cols * depth,
            bytes_accessed=4 * (rows * depth + depth * cols + 2 * rows * cols),
            transcendentals=0,
        ),
        name="product",
    )(*args)


def per_device(a_blocks, a_rows, a_cols, a_counts, b_blocks, b_rows, b_cols, b_counts, out_mask):
    row_now = lax.axis_index("row")
    col_now = lax.axis_index("col")
    z_now = row_now % NZ
    y_now, x_now, c_now = col_now // (NX * NC), col_now // NC % NX, col_now % NC

    b_send = pack_b(
        z_now.reshape(1), b_counts.reshape(-1), b_cols.reshape(-1), b_blocks.reshape(-1, BS, BS)
    )
    a_send = pack_a(a_counts.reshape(-1), a_rows.reshape(-1), a_blocks.reshape(-1, BS, BS))
    b_got = [b_send[0]] + [row_shift(b_send[rel], dz=rel) for rel in range(1, NZ)]
    a_got = lax.all_to_all(a_send, "col", split_axis=0, concat_axis=0, tiled=True)

    b_part = unpack_b(b_got)
    b_here = b_part + row_shift(b_part, dy=1)
    half = KZ * BS // 2
    b_behind = row_shift(b_here, dz=1)
    b_ahead = row_shift(b_here, dz=-1)
    b_far_lo = row_shift(b_behind[:half], dz=1)
    b_far_hi = row_shift(b_ahead[half:], dz=-1)

    def swap(value):
        return col_shift(value, dc=1)

    half = RB * BS // 2
    plane = []
    own = unpack_a(a_got)
    other = col_shift(own, dy=1)
    for first in (own, other):
        behind = col_shift(first, dx=1)
        ahead = col_shift(first, dx=-1)
        far_lo = col_shift(behind[:half], dx=1)
        far_hi = col_shift(ahead[half:], dx=-1)
        plane.append((first, behind, ahead, far_lo, far_hi))

    def pairs(values):
        return [v for value in values for v in (value, swap(value))]

    def far_pairs(lo, hi):
        return [(lo, hi), (swap(lo), swap(hi))]

    def k_of(dy, dx):
        return [col_id(y_now + dy, x_now + dx, c_now + dc) for dc in (0, 1)]

    near = (0, -1, 1)
    order = [k for dx in near for k in k_of(0, dx)] + k_of(0, 2)
    order += [k for dx in near for k in k_of(1, dx)] + k_of(1, 2)
    order = jnp.stack(order + [z_now]).astype(jnp.int32)
    b_all = order_b(order, (b_here, b_ahead, b_behind, b_far_lo, b_far_hi))

    total = product(pairs(plane[0][:3]), far_pairs(*plane[0][3:]), b_all[0])
    total = product(pairs(plane[1][:3]), [], b_all[1], before=total)
    return product([], far_pairs(*plane[1][3:]), b_all[2], before=total, mask=out_mask)


def solution(mesh):
    lists = P("row", "col", None)
    blocks = P("row", "col", None, None, None)
    in_specs = (blocks, lists, lists, lists, blocks, lists, lists, lists, P("row", "col"))
    return jax.shard_map(
        per_device, mesh=mesh, in_specs=in_specs, out_specs=P("row", "col"), check_vma=False
    )
```

```python
import functools

import jax
import jax.numpy as jnp
from jax import lax
from jax.experimental import pallas as pl
from jax.experimental.pallas import tpu as pltpu
from jax.sharding import PartitionSpec as P

BS = 128
CAP = 2
NX, NY, NC, NZ = 4, 2, 2, 4
N_COL = NY * NX * NC
N_ROW = 2 * NZ
KB = 16
KZ = KB // NZ
RB = 16
CB = 4
MET = 8
F32 = jnp.float32
ANY = pl.BlockSpec(memory_space=pl.ANY)
HBM = pl.BlockSpec(memory_space=pltpu.HBM)
SMEM = pl.BlockSpec(memory_space=pltpu.SMEM)
VMEM = pl.BlockSpec(memory_space=pltpu.VMEM)


def col_id(y, x, c):
    return (y % NY) * NX * NC + (x % NX) * NC + c % NC


def col_shift(value, dy=0, dx=0, dc=0, by_core=False):
    route = [
        (col_id(y, x, c), col_id(y + dy, x + (dx if c == 0 or not by_core else -dx), c + dc))
        for y in range(NY)
        for x in range(NX)
        for c in range(NC)
    ]
    return lax.ppermute(value, "col", route)


def row_shift(value, dy=0, dz=0):
    route = [
        (y * NZ + z, (y + dy) % 2 * NZ + (z + dz) % NZ) for y in range(2) for z in range(NZ)
    ]
    return lax.ppermute(value, "row", route)


def row_shift_by_core(value, dz):
    route = []
    for i in range(N_ROW):
        for j in range(N_COL):
            step = dz if j % NC == 0 else -dz
            route.append((i * N_COL + j, (i // NZ * NZ + (i + step) % NZ) * N_COL + j))
    return lax.ppermute(value, ("row", "col"), route)


def after(value, *others):
    return lax.optimization_barrier((value, *others))[0]


def place():
    row, col = lax.axis_index("row"), lax.axis_index("col")
    core = lax.rem(col, NC)
    return (
        lax.rem(row, NZ),
        lax.div(col, NX * NC),
        lax.rem(lax.div(col, NC), NX),
        core,
        1 - 2 * core,
    )


def lane_marks(first, second):
    lane = lax.broadcasted_iota(jnp.int32, (MET, BS), 1)
    marks = jnp.where(lane == 0, first, jnp.where(lane == 1, second, -1))
    return marks.astype(F32)


def pack_a_kernel(counts, owners, blocks, send, sems):
    start = jnp.int32(0)
    jobs = []
    for k in range(KB):
        count = counts[k]
        places = []
        for rank in range(CAP):
            slot = jnp.minimum(start + rank, blocks.shape[0] - 1)
            copy = pltpu.make_async_copy(
                blocks.at[slot], send.at[k, pl.ds(rank * BS, BS)], sems.at[k, rank]
            )
            have = count > rank
            pl.when(have)(copy.start)
            jobs.append((have, copy))
            places.append(jnp.where(have, lax.rem(owners[slot], RB), -1))
        send[k, pl.ds(CAP * BS, MET)] = lane_marks(*places)
        start = start + count
    for have, copy in jobs:
        pl.when(have)(copy.wait)


def pack_a(counts, owners, blocks):
    return pl.pallas_call(
        pack_a_kernel,
        out_shape=jax.ShapeDtypeStruct((N_COL, CAP * BS + MET, BS), F32),
        in_specs=[SMEM, SMEM, ANY],
        out_specs=VMEM,
        scratch_shapes=[pltpu.SemaphoreType.DMA((KB, CAP))],
        name="pack_a",
    )(counts, owners, blocks)


def pack_b_kernel(counts, owners, blocks, *rest):
    sends, (starts, sems) = rest[:NZ], rest[NZ:]
    start = jnp.int32(0)
    for k in range(KB):
        starts[k] = start
        start = start + counts[k]
    jobs = []
    for rel in range(NZ):
        base = lax.rem(place()[0] + rel, NZ) * KZ
        for kk in range(KZ):
            count = counts[base + kk]
            places = []
            for rank in range(CAP):
                slot = jnp.minimum(starts[base + kk] + rank, blocks.shape[0] - 1)
                piece = kk * CAP + rank
                copy = pltpu.make_async_copy(
                    blocks.at[slot], sends[rel].at[pl.ds(piece * BS, BS)], sems.at[rel, piece]
                )
                have = count > rank
                pl.when(have)(copy.start)
                jobs.append((have, copy))
                places.append(jnp.where(have, lax.rem(owners[slot], CB), -1))
            sends[rel][pl.ds(KZ * CAP * BS + kk * MET, MET)] = lane_marks(*places)
    for have, copy in jobs:
        pl.when(have)(copy.wait)


def pack_b(counts, owners, blocks):
    rows = KZ * (CAP * BS + MET)
    return pl.pallas_call(
        pack_b_kernel,
        out_shape=[jax.ShapeDtypeStruct((rows, BS), F32)] * NZ,
        in_specs=[SMEM, SMEM, ANY],
        out_specs=[VMEM] * NZ,
        scratch_shapes=[
            pltpu.SMEM((KB,), jnp.int32),
            pltpu.SemaphoreType.DMA((NZ, KZ * CAP)),
        ],
        name="pack_b",
    )(counts, owners, blocks)


def unpack_a_kernel(got, panel, marks, sems, mark_sem):
    read = pltpu.make_async_copy(got.at[:, CAP * BS], marks, mark_sem)
    read.start()
    panel[...] = jnp.zeros_like(panel)
    read.wait()
    jobs = []
    for source in range(N_COL):
        for rank in range(CAP):
            place = marks[source, rank].astype(jnp.int32)
            have = place >= 0
            at = pl.multiple_of(jnp.maximum(place, 0) * BS, BS)
            copy = pltpu.make_async_copy(
                got.at[source, pl.ds(rank * BS, BS)], panel.at[pl.ds(at, BS)], sems.at[source, rank]
            )
            pl.when(have)(copy.start)
            jobs.append((have, copy))
    for have, copy in jobs:
        pl.when(have)(copy.wait)


def unpack_a(got):
    return pl.pallas_call(
        unpack_a_kernel,
        out_shape=jax.ShapeDtypeStruct((RB * BS, BS), F32),
        in_specs=[HBM],
        out_specs=VMEM,
        scratch_shapes=[
            pltpu.SMEM((N_COL, BS), F32),
            pltpu.SemaphoreType.DMA((N_COL, CAP)),
            pltpu.SemaphoreType.DMA,
        ],
        name="unpack_a",
    )(got)


def unpack_b_kernel(*refs):
    gots, (panel, marks, sems, mark_sem) = refs[:NZ], refs[NZ:]
    reads = []
    for rel in range(NZ):
        read = pltpu.make_async_copy(
            gots[rel].at[pl.ds(KZ * CAP * BS, KZ * MET)], marks.at[rel], mark_sem.at[rel]
        )
        read.start()
        reads.append(read)
    panel[...] = jnp.zeros_like(panel)
    for read in reads:
        read.wait()
    jobs = []
    for rel in range(NZ):
        for kk in range(KZ):
            for rank in range(CAP):
                place = marks[rel, kk * MET, rank].astype(jnp.int32)
                have = place >= 0
                at = pl.multiple_of(jnp.maximum(place, 0) * BS, BS)
                piece = kk * CAP + rank
                copy = pltpu.make_async_copy(
                    gots[rel].at[pl.ds(piece * BS, BS)],
                    panel.at[pl.ds(kk * BS, BS), pl.ds(at, BS)],
                    sems.at[rel, piece],
                )
                pl.when(have)(copy.start)
                jobs.append((have, copy))
    for have, copy in jobs:
        pl.when(have)(copy.wait)


def unpack_b(gots):
    return pl.pallas_call(
        unpack_b_kernel,
        out_shape=jax.ShapeDtypeStruct((KZ * BS, CB * BS), F32),
        in_specs=[HBM] * NZ,
        out_specs=VMEM,
        scratch_shapes=[
            pltpu.SMEM((NZ, KZ * MET, BS), F32),
            pltpu.SemaphoreType.DMA((NZ, KZ * CAP)),
            pltpu.SemaphoreType.DMA((NZ,)),
        ],
        name="unpack_b",
    )(*gots)


def split(value):
    high = value.astype(jnp.bfloat16)
    return high, (value - high.astype(F32)).astype(jnp.bfloat16)


def k_order():
    _, y, x, c, step = place()
    ks = []
    for dy in range(NY):
        y_at = lax.rem(y + dy, NY)
        for dx in (0, -step, step, 2):
            for dc in range(NC):
                x_at = lax.rem(x + NX + (dx if dc == 0 or isinstance(dx, int) else -dx), NX)
                ks.append(y_at * (NX * NC) + x_at * NC + lax.rem(c + dc, NC))
    return ks


TM = 512


def product_kernel(mask, here, first, second, far, *rest):
    pieces, (out, panel, stack, sems) = rest[:KB], rest[KB:]
    tile = pl.program_id(0)

    @pl.when(tile == 0)
    def _():
        z_now, step = place()[0], place()[4]
        jobs = []
        for p, k in enumerate(k_order()):
            hop = lax.rem((z_now - lax.div(k, KZ)) * step + 2 * NZ, NZ)
            row = pl.multiple_of(lax.rem(k, KZ) * BS, BS)
            for want, source in ((0, here), (1, first), (2, far), (3, second)):
                copy = pltpu.make_async_copy(
                    source.at[pl.ds(row, BS)], panel.at[pl.ds(p * BS, BS)], sems.at[p]
                )
                pl.when(hop == want)(copy.start)
            jobs.append(copy)
        for p, job in enumerate(jobs):
            job.wait()
            high, low = split(panel[pl.ds(p * BS, BS), :])
            stack[pl.ds(p * BS, BS), :] = high
            stack[pl.ds((KB + p) * BS, BS), :] = low

    high, low = split(jnp.concatenate([ref[...] for ref in pieces], axis=1))
    total = jnp.dot(
        jnp.concatenate([high, high], axis=1), stack[...], preferred_element_type=F32
    )
    total += jnp.dot(low, stack[pl.ds(0, KB * BS), :], preferred_element_type=F32)
    for r in range(TM // BS):
        for c in range(CB):
            keep = mask[tile * (TM // BS) + r, c].astype(F32)
            piece = total[r * BS : (r + 1) * BS, c * BS : (c + 1) * BS]
            out[pl.ds(r * BS, BS), pl.ds(c * BS, BS)] = piece * keep


def product(mask, b_pieces, a_pieces):
    rows, cols = RB * BS, CB * BS
    return pl.pallas_call(
        product_kernel,
        grid=(rows // TM,),
        out_shape=jax.ShapeDtypeStruct((rows, cols), F32),
        in_specs=[SMEM]
        + [ANY] * len(b_pieces)
        + [pl.BlockSpec((TM, BS), lambda t: (t, 0))] * len(a_pieces),
        out_specs=pl.BlockSpec((TM, cols), lambda t: (t, 0)),
        scratch_shapes=[
            pltpu.VMEM((KB * BS, cols), F32),
            pltpu.VMEM((2 * KB * BS, cols), jnp.bfloat16),
            pltpu.SemaphoreType.DMA((KB,)),
        ],
        compiler_params=pltpu.CompilerParams(vmem_limit_bytes=48 << 20),
        name="product",
    )(mask, *b_pieces, *a_pieces)


def per_device(a_blocks, a_rows, a_cols, a_counts, b_blocks, b_rows, b_cols, b_counts, out_mask):
    a_send = pack_a(a_counts.reshape(-1), a_rows.reshape(-1), a_blocks.reshape(-1, BS, BS))
    a_got = lax.all_to_all(a_send, "col", split_axis=0, concat_axis=0, tiled=True)
    b_send = pack_b(
        after(b_counts.reshape(-1), a_send), b_cols.reshape(-1), b_blocks.reshape(-1, BS, BS)
    )
    b_got = [b_send[0]] + [row_shift(b_send[rel], dz=rel) for rel in range(1, NZ)]
    b_part = unpack_b(b_got)
    own = unpack_a(a_got)
    joined = lax.optimization_barrier

    def swap(value, *earlier):
        return col_shift(after(value, *earlier) if earlier else value, dc=1)

    def hop(value, step):
        return col_shift(value, dx=step, by_core=True)

    own_first, own_second, other = hop(own, 1), hop(own, -1), col_shift(own, dy=1)
    own_first, own_second = joined((own_first, own_second))
    own_far = hop(own_first, 1)
    b_here = b_part + after(row_shift(b_part, dy=1), own_first)
    b_first, b_second = row_shift_by_core(b_here, 1), row_shift_by_core(b_here, -1)
    b_far = row_shift_by_core(b_first, 1)
    other_first, other_second = hop(other, 1), hop(other, -1)
    other_far = hop(other_first, 1)

    a_all = []
    for value in (own, own_first, own_second, own_far):
        a_all += [value, swap(value)]
    for value in (other, other_first, other_second, other_far):
        a_all += [value, swap(value)]
    return product(out_mask, (b_here, b_first, b_second, b_far), a_all)


def solution(mesh):
    lists = P("row", "col", None)
    blocks = P("row", "col", None, None, None)
    in_specs = (blocks, lists, lists, lists, blocks, lists, lists, lists, P("row", "col"))
    return jax.shard_map(
        per_device, mesh=mesh, in_specs=in_specs, out_specs=P("row", "col"), check_vma=False
    )
```

```python
import functools

import jax
import jax.numpy as jnp
from jax import lax
from jax.experimental import pallas as pl
from jax.experimental.pallas import tpu as pltpu
from jax.sharding import PartitionSpec as P

BS = 128
CAP = 2
NX, NY, NC, NZ = 4, 2, 2, 4
N_COL = NY * NX * NC
N_ROW = 2 * NZ
KB = 16
KZ = KB // NZ
RB = 16
CB = 4
MET = 8
F32 = jnp.float32
ANY = pl.BlockSpec(memory_space=pl.ANY)
HBM = pl.BlockSpec(memory_space=pltpu.HBM)
SMEM = pl.BlockSpec(memory_space=pltpu.SMEM)
VMEM = pl.BlockSpec(memory_space=pltpu.VMEM)


def col_id(y, x, c):
    return (y % NY) * NX * NC + (x % NX) * NC + c % NC


def col_shift(value, dy=0, dx=0, dc=0, by_core=False):
    route = [
        (col_id(y, x, c), col_id(y + dy, x + (dx if c == 0 or not by_core else -dx), c + dc))
        for y in range(NY)
        for x in range(NX)
        for c in range(NC)
    ]
    return lax.ppermute(value, "col", route)


def row_shift(value, dy=0, dz=0):
    route = [
        (y * NZ + z, (y + dy) % 2 * NZ + (z + dz) % NZ) for y in range(2) for z in range(NZ)
    ]
    return lax.ppermute(value, "row", route)


def row_shift_by_core(value, dz):
    route = []
    for i in range(N_ROW):
        for j in range(N_COL):
            step = dz if j % NC == 0 else -dz
            route.append((i * N_COL + j, (i // NZ * NZ + (i + step) % NZ) * N_COL + j))
    return lax.ppermute(value, ("row", "col"), route)


def after(value, *others):
    return lax.optimization_barrier((value, *others))[0]


def place():
    row, col = lax.axis_index("row"), lax.axis_index("col")
    core = lax.rem(col, NC)
    return (
        lax.rem(row, NZ),
        lax.div(col, NX * NC),
        lax.rem(lax.div(col, NC), NX),
        core,
        1 - 2 * core,
    )


def lane_marks(first, second):
    lane = lax.broadcasted_iota(jnp.int32, (MET, BS), 1)
    marks = jnp.where(lane == 0, first, jnp.where(lane == 1, second, -1))
    return marks.astype(F32)


def pack_a_kernel(counts, owners, blocks, send, sems):
    start = jnp.int32(0)
    jobs = []
    for k in range(KB):
        count = counts[k]
        places = []
        for rank in range(CAP):
            slot = jnp.minimum(start + rank, blocks.shape[0] - 1)
            copy = pltpu.make_async_copy(
                blocks.at[slot], send.at[k, pl.ds(rank * BS, BS)], sems.at[k, rank]
            )
            have = count > rank
            pl.when(have)(copy.start)
            jobs.append((have, copy))
            places.append(jnp.where(have, lax.rem(owners[slot], RB), -1))
        send[k, pl.ds(CAP * BS, MET)] = lane_marks(*places)
        start = start + count
    for have, copy in jobs:
        pl.when(have)(copy.wait)


def pack_a(counts, owners, blocks):
    return pl.pallas_call(
        pack_a_kernel,
        out_shape=jax.ShapeDtypeStruct((N_COL, CAP * BS + MET, BS), F32),
        in_specs=[SMEM, SMEM, ANY],
        out_specs=VMEM,
        scratch_shapes=[pltpu.SemaphoreType.DMA((KB, CAP))],
        name="pack_a",
    )(counts, owners, blocks)


def pack_b_kernel(counts, owners, blocks, *rest):
    sends, (starts, sems) = rest[:NZ], rest[NZ:]
    start = jnp.int32(0)
    for k in range(KB):
        starts[k] = start
        start = start + counts[k]
    jobs = []
    for rel in range(NZ):
        base = lax.rem(place()[0] + rel, NZ) * KZ
        for kk in range(KZ):
            count = counts[base + kk]
            places = []
            for rank in range(CAP):
                slot = jnp.minimum(starts[base + kk] + rank, blocks.shape[0] - 1)
                piece = kk * CAP + rank
                copy = pltpu.make_async_copy(
                    blocks.at[slot], sends[rel].at[pl.ds(piece * BS, BS)], sems.at[rel, piece]
                )
                have = count > rank
                pl.when(have)(copy.start)
                jobs.append((have, copy))
                places.append(jnp.where(have, lax.rem(owners[slot], CB), -1))
            sends[rel][pl.ds(KZ * CAP * BS + kk * MET, MET)] = lane_marks(*places)
    for have, copy in jobs:
        pl.when(have)(copy.wait)


def pack_b(counts, owners, blocks):
    rows = KZ * (CAP * BS + MET)
    return pl.pallas_call(
        pack_b_kernel,
        out_shape=[jax.ShapeDtypeStruct((rows, BS), F32)] * NZ,
        in_specs=[SMEM, SMEM, ANY],
        out_specs=[VMEM] * NZ,
        scratch_shapes=[
            pltpu.SMEM((KB,), jnp.int32),
            pltpu.SemaphoreType.DMA((NZ, KZ * CAP)),
        ],
        name="pack_b",
    )(counts, owners, blocks)


def unpack_a_kernel(got, panel, marks, sems, mark_sem):
    read = pltpu.make_async_copy(got.at[:, CAP * BS], marks, mark_sem)
    read.start()
    panel[...] = jnp.zeros_like(panel)
    read.wait()
    jobs = []
    for source in range(N_COL):
        for rank in range(CAP):
            place = marks[source, rank].astype(jnp.int32)
            have = place >= 0
            at = pl.multiple_of(jnp.maximum(place, 0) * BS, BS)
            copy = pltpu.make_async_copy(
                got.at[source, pl.ds(rank * BS, BS)], panel.at[pl.ds(at, BS)], sems.at[source, rank]
            )
            pl.when(have)(copy.start)
            jobs.append((have, copy))
    for have, copy in jobs:
        pl.when(have)(copy.wait)


def unpack_a(got):
    return pl.pallas_call(
        unpack_a_kernel,
        out_shape=jax.ShapeDtypeStruct((RB * BS, BS), F32),
        in_specs=[HBM],
        out_specs=VMEM,
        scratch_shapes=[
            pltpu.SMEM((N_COL, BS), F32),
            pltpu.SemaphoreType.DMA((N_COL, CAP)),
            pltpu.SemaphoreType.DMA,
        ],
        name="unpack_a",
    )(got)


def unpack_b_kernel(*refs):
    gots, (panel, marks, sems, mark_sem) = refs[:NZ], refs[NZ:]
    reads = []
    for rel in range(NZ):
        read = pltpu.make_async_copy(
            gots[rel].at[pl.ds(KZ * CAP * BS, KZ * MET)], marks.at[rel], mark_sem.at[rel]
        )
        read.start()
        reads.append(read)
    panel[...] = jnp.zeros_like(panel)
    for read in reads:
        read.wait()
    jobs = []
    for rel in range(NZ):
        for kk in range(KZ):
            for rank in range(CAP):
                place = marks[rel, kk * MET, rank].astype(jnp.int32)
                have = place >= 0
                at = pl.multiple_of(jnp.maximum(place, 0) * BS, BS)
                piece = kk * CAP + rank
                copy = pltpu.make_async_copy(
                    gots[rel].at[pl.ds(piece * BS, BS)],
                    panel.at[pl.ds(kk * BS, BS), pl.ds(at, BS)],
                    sems.at[rel, piece],
                )
                pl.when(have)(copy.start)
                jobs.append((have, copy))
    for have, copy in jobs:
        pl.when(have)(copy.wait)


def unpack_b(gots):
    return pl.pallas_call(
        unpack_b_kernel,
        out_shape=jax.ShapeDtypeStruct((KZ * BS, CB * BS), F32),
        in_specs=[HBM] * NZ,
        out_specs=VMEM,
        scratch_shapes=[
            pltpu.SMEM((NZ, KZ * MET, BS), F32),
            pltpu.SemaphoreType.DMA((NZ, KZ * CAP)),
            pltpu.SemaphoreType.DMA((NZ,)),
        ],
        name="unpack_b",
    )(*gots)


def split(value):
    high = value.astype(jnp.bfloat16)
    return high, (value - high.astype(F32)).astype(jnp.bfloat16)


def k_order():
    _, y, x, c, step = place()
    ks = []
    for dy in range(NY):
        y_at = lax.rem(y + dy, NY)
        for dx in (0, -step, step, 2):
            for dc in range(NC):
                x_at = lax.rem(x + NX + (dx if dc == 0 or isinstance(dx, int) else -dx), NX)
                ks.append(y_at * (NX * NC) + x_at * NC + lax.rem(c + dc, NC))
    return ks


TM = 512


def product_kernel(last, mask, *refs):
    refs = list(refs)
    b_pieces = [refs.pop(0) for _ in range(1 if last else NZ - 1)]
    pieces = [refs.pop(0) for _ in range(KB)]
    before = refs.pop(0) if last else None
    out, rows, panel, stack, a_sems, b_sems = refs
    tile, tiles = pl.program_id(0), pl.num_programs(0)
    depth = len(b_pieces) * KZ * BS
    z_now, step = place()[0], place()[4]

    def fetch(at, wait):
        buffer = lax.rem(at, 2)
        for piece, k in zip(pieces, k_order()):
            hop = lax.rem((z_now - lax.div(k, KZ)) * step + 2 * NZ, NZ)
            slot = lax.rem(k, KZ) + (0 if last else KZ * jnp.minimum(hop, 2))
            copy = pltpu.make_async_copy(
                piece.at[pl.ds(pl.multiple_of(at * TM, TM), TM)],
                rows.at[buffer, :, pl.ds(pl.multiple_of(slot * BS, BS), BS)],
                a_sems.at[buffer, slot],
            )
            pl.when(hop == 2 if last else hop != 2)(copy.wait if wait else copy.start)

    @pl.when(tile == 0)
    def _():
        jobs = [
            pltpu.make_async_copy(piece, panel.at[pl.ds(i * KZ * BS, KZ * BS)], b_sems.at[i])
            for i, piece in enumerate(b_pieces)
        ]
        for job in jobs:
            job.start()
        fetch(tile, False)
        fetch(tile + 1, False)
        for job in jobs:
            job.wait()
        high, low = split(panel[...])
        stack[pl.ds(0, depth), :] = high
        stack[pl.ds(depth, depth), :] = low

    fetch(tile, True)
    high, low = split(rows[lax.rem(tile, 2)])
    total = jnp.dot(
        jnp.concatenate([high, high], axis=1), stack[...], preferred_element_type=F32
    )
    total += jnp.dot(low, stack[pl.ds(0, depth), :], preferred_element_type=F32)
    if last:
        total += before[...]
        for r in range(TM // BS):
            for c in range(CB):
                keep = mask[tile * (TM // BS) + r, c].astype(F32)
                piece = total[r * BS : (r + 1) * BS, c * BS : (c + 1) * BS]
                out[pl.ds(r * BS, BS), pl.ds(c * BS, BS)] = piece * keep
    else:
        out[...] = total
    pl.when(tile + 2 < tiles)(lambda: fetch(tile + 2, False))


def product(mask, b_pieces, a_pieces, before=None):
    height, cols = RB * BS, CB * BS
    depth = len(b_pieces) * KZ * BS
    c_spec = pl.BlockSpec((TM, cols), lambda t: (t, 0))
    last = before is not None
    return pl.pallas_call(
        functools.partial(product_kernel, last),
        grid=(height // TM,),
        out_shape=jax.ShapeDtypeStruct((height, cols), F32),
        in_specs=[SMEM] + [HBM] * (len(b_pieces) + KB) + [c_spec] * last,
        out_specs=c_spec,
        scratch_shapes=[
            pltpu.VMEM((2, TM, depth), F32),
            pltpu.VMEM((depth, cols), F32),
            pltpu.VMEM((2 * depth, cols), jnp.bfloat16),
            pltpu.SemaphoreType.DMA((2, depth // BS)),
            pltpu.SemaphoreType.DMA((len(b_pieces),)),
        ],
        compiler_params=pltpu.CompilerParams(vmem_limit_bytes=58 << 20),
        cost_estimate=pl.CostEstimate(
            flops=6 * height * cols * depth,
            bytes_accessed=4 * (height * depth + depth * cols + 2 * height * cols),
            transcendentals=0,
        ),
        name="product",
    )(mask, *b_pieces, *a_pieces, *([before] if last else []))


def per_device(a_blocks, a_rows, a_cols, a_counts, b_blocks, b_rows, b_cols, b_counts, out_mask):
    a_send = pack_a(a_counts.reshape(-1), a_rows.reshape(-1), a_blocks.reshape(-1, BS, BS))
    a_got = lax.all_to_all(a_send, "col", split_axis=0, concat_axis=0, tiled=True)
    b_send = pack_b(
        after(b_counts.reshape(-1), a_send), b_cols.reshape(-1), b_blocks.reshape(-1, BS, BS)
    )
    b_got = [b_send[0]] + [row_shift(b_send[rel], dz=rel) for rel in range(1, NZ)]
    b_part = unpack_b(b_got)
    own = unpack_a(a_got)
    joined = lax.optimization_barrier

    def swap(value, *earlier):
        return col_shift(after(value, *earlier) if earlier else value, dc=1)

    def hop(value, step):
        return col_shift(value, dx=step, by_core=True)

    with jax.named_scope("t_F"):
        v_F = hop(own, 1)
    with jax.named_scope("t_S"):
        v_S = row_shift(b_part, dy=1)
    with jax.named_scope("t_G"):
        v_G = hop(own, -1)
    with jax.named_scope("t_H"):
        v_H = hop(after(v_F, v_G), 1)
    with jax.named_scope("t_cown"):
        v_cown = swap(after(own, v_G))
    with jax.named_scope("t_Y"):
        v_Y = col_shift(own, dy=1)
    with jax.named_scope("t_cF"):
        v_cF = swap(v_F)
    with jax.named_scope("t_cY"):
        v_cY = swap(after(v_Y, v_G))
    with jax.named_scope("t_cH"):
        v_cH = swap(v_H)
    with jax.named_scope("t_cG"):
        v_cG = swap(v_G)
    with jax.named_scope("t_YF"):
        v_YF = hop(after(v_Y, v_G), 1)
    with jax.named_scope("t_YG"):
        v_YG = hop(v_Y, -1)
    with jax.named_scope("t_cYF"):
        v_cYF = swap(after(v_YF, v_cown))
    with jax.named_scope("t_cYG"):
        v_cYG = swap(v_YG)
    v_b_here = b_part + after(v_S, v_F)
    with jax.named_scope("t_YH"):
        v_YH = hop(after(v_YF, v_YF), 1)
    with jax.named_scope("t_bG"):
        v_bG = row_shift_by_core(v_b_here, -1)
    with jax.named_scope("t_bF"):
        v_bF = row_shift_by_core(v_b_here, 1)
    with jax.named_scope("t_bH"):
        v_bH = row_shift_by_core(after(v_bF, v_G), 1)
    with jax.named_scope("t_cYH"):
        v_cYH = swap(v_YH)
    b_all = (v_b_here, v_bF, v_bG, v_bH)
    a_all = [own, v_cown, v_F, v_cF, v_G, v_cG, v_H, v_cH]
    a_all += [v_Y, v_cY, v_YF, v_cYF, v_YG, v_cYG, v_YH, v_cYH]
    total = product(out_mask, b_all[:3], a_all)
    return product(out_mask, b_all[3:], a_all, before=total)


def solution(mesh):
    lists = P("row", "col", None)
    blocks = P("row", "col", None, None, None)
    in_specs = (blocks, lists, lists, lists, blocks, lists, lists, lists, P("row", "col"))
    return jax.shard_map(
        per_device, mesh=mesh, in_specs=in_specs, out_specs=P("row", "col"), check_vma=False
    )
```

```python
import functools

import jax
import jax.numpy as jnp
from jax import lax
from jax.experimental import pallas as pl
from jax.experimental.pallas import tpu as pltpu
from jax.sharding import PartitionSpec as P

BS = 128
CAP = 2
NX, NY, NC, NZ = 4, 2, 2, 4
N_COL = NY * NX * NC
N_ROW = 2 * NZ
KB = 16
KZ = KB // NZ
RB = 16
CB = 4
MET = 8
F32 = jnp.float32
ANY = pl.BlockSpec(memory_space=pl.ANY)
HBM = pl.BlockSpec(memory_space=pltpu.HBM)
SMEM = pl.BlockSpec(memory_space=pltpu.SMEM)
VMEM = pl.BlockSpec(memory_space=pltpu.VMEM)


def col_id(y, x, c):
    return (y % NY) * NX * NC + (x % NX) * NC + c % NC


def col_shift(value, dy=0, dx=0, dc=0, by_core=False):
    route = [
        (col_id(y, x, c), col_id(y + dy, x + (dx if c == 0 or not by_core else -dx), c + dc))
        for y in range(NY)
        for x in range(NX)
        for c in range(NC)
    ]
    return lax.ppermute(value, "col", route)


def row_shift(value, dy=0, dz=0):
    route = [
        (y * NZ + z, (y + dy) % 2 * NZ + (z + dz) % NZ) for y in range(2) for z in range(NZ)
    ]
    return lax.ppermute(value, "row", route)


def row_shift_by_core(value, dz):
    route = []
    for i in range(N_ROW):
        for j in range(N_COL):
            step = dz if j % NC == 0 else -dz
            route.append((i * N_COL + j, (i // NZ * NZ + (i + step) % NZ) * N_COL + j))
    return lax.ppermute(value, ("row", "col"), route)


def after(value, *others):
    return lax.optimization_barrier((value, *others))[0]


def place():
    row, col = lax.axis_index("row"), lax.axis_index("col")
    core = lax.rem(col, NC)
    return (
        lax.rem(row, NZ),
        lax.div(col, NX * NC),
        lax.rem(lax.div(col, NC), NX),
        core,
        1 - 2 * core,
    )


def lane_marks(first, second):
    lane = lax.broadcasted_iota(jnp.int32, (MET, BS), 1)
    marks = jnp.where(lane == 0, first, jnp.where(lane == 1, second, -1))
    return marks.astype(F32)


def pack_a_kernel(counts, owners, blocks, send, sems):
    start = jnp.int32(0)
    jobs = []
    for k in range(KB):
        count = counts[k]
        places = []
        for rank in range(CAP):
            slot = jnp.minimum(start + rank, blocks.shape[0] - 1)
            copy = pltpu.make_async_copy(
                blocks.at[slot], send.at[k, pl.ds(rank * BS, BS)], sems.at[k, rank]
            )
            have = count > rank
            pl.when(have)(copy.start)
            jobs.append((have, copy))
            places.append(jnp.where(have, lax.rem(owners[slot], RB), -1))
        send[k, pl.ds(CAP * BS, MET)] = lane_marks(*places)
        start = start + count
    for have, copy in jobs:
        pl.when(have)(copy.wait)


def pack_a(counts, owners, blocks):
    return pl.pallas_call(
        pack_a_kernel,
        out_shape=jax.ShapeDtypeStruct((N_COL, CAP * BS + MET, BS), F32),
        in_specs=[SMEM, SMEM, ANY],
        out_specs=VMEM,
        scratch_shapes=[pltpu.SemaphoreType.DMA((KB, CAP))],
        name="pack_a",
    )(counts, owners, blocks)


def pack_b_kernel(counts, owners, blocks, *rest):
    sends, (starts, sems) = rest[:NZ], rest[NZ:]
    start = jnp.int32(0)
    for k in range(KB):
        starts[k] = start
        start = start + counts[k]
    jobs = []
    for rel in range(NZ):
        base = lax.rem(place()[0] + rel, NZ) * KZ
        for kk in range(KZ):
            count = counts[base + kk]
            places = []
            for rank in range(CAP):
                slot = jnp.minimum(starts[base + kk] + rank, blocks.shape[0] - 1)
                piece = kk * CAP + rank
                copy = pltpu.make_async_copy(
                    blocks.at[slot], sends[rel].at[pl.ds(piece * BS, BS)], sems.at[rel, piece]
                )
                have = count > rank
                pl.when(have)(copy.start)
                jobs.append((have, copy))
                places.append(jnp.where(have, lax.rem(owners[slot], CB), -1))
            sends[rel][pl.ds(KZ * CAP * BS + kk * MET, MET)] = lane_marks(*places)
    for have, copy in jobs:
        pl.when(have)(copy.wait)


def pack_b(counts, owners, blocks):
    rows = KZ * (CAP * BS + MET)
    return pl.pallas_call(
        pack_b_kernel,
        out_shape=[jax.ShapeDtypeStruct((rows, BS), F32)] * NZ,
        in_specs=[SMEM, SMEM, ANY],
        out_specs=[VMEM] * NZ,
        scratch_shapes=[
            pltpu.SMEM((KB,), jnp.int32),
            pltpu.SemaphoreType.DMA((NZ, KZ * CAP)),
        ],
        name="pack_b",
    )(counts, owners, blocks)


def unpack_a_kernel(got, panel, marks, sems, mark_sem):
    read = pltpu.make_async_copy(got.at[:, CAP * BS], marks, mark_sem)
    read.start()
    panel[...] = jnp.zeros_like(panel)
    read.wait()
    jobs = []
    for source in range(N_COL):
        for rank in range(CAP):
            place = marks[source, rank].astype(jnp.int32)
            have = place >= 0
            at = pl.multiple_of(jnp.maximum(place, 0) * BS, BS)
            copy = pltpu.make_async_copy(
                got.at[source, pl.ds(rank * BS, BS)], panel.at[pl.ds(at, BS)], sems.at[source, rank]
            )
            pl.when(have)(copy.start)
            jobs.append((have, copy))
    for have, copy in jobs:
        pl.when(have)(copy.wait)


def unpack_a(got):
    return pl.pallas_call(
        unpack_a_kernel,
        out_shape=jax.ShapeDtypeStruct((RB * BS, BS), F32),
        in_specs=[HBM],
        out_specs=VMEM,
        scratch_shapes=[
            pltpu.SMEM((N_COL, BS), F32),
            pltpu.SemaphoreType.DMA((N_COL, CAP)),
            pltpu.SemaphoreType.DMA,
        ],
        name="unpack_a",
    )(got)


def unpack_b_kernel(*refs):
    gots, (panel, marks, sems, mark_sem) = refs[:NZ], refs[NZ:]
    reads = []
    for rel in range(NZ):
        read = pltpu.make_async_copy(
            gots[rel].at[pl.ds(KZ * CAP * BS, KZ * MET)], marks.at[rel], mark_sem.at[rel]
        )
        read.start()
        reads.append(read)
    panel[...] = jnp.zeros_like(panel)
    for read in reads:
        read.wait()
    jobs = []
    for rel in range(NZ):
        for kk in range(KZ):
            for rank in range(CAP):
                place = marks[rel, kk * MET, rank].astype(jnp.int32)
                have = place >= 0
                at = pl.multiple_of(jnp.maximum(place, 0) * BS, BS)
                piece = kk * CAP + rank
                copy = pltpu.make_async_copy(
                    gots[rel].at[pl.ds(piece * BS, BS)],
                    panel.at[pl.ds(kk * BS, BS), pl.ds(at, BS)],
                    sems.at[rel, piece],
                )
                pl.when(have)(copy.start)
                jobs.append((have, copy))
    for have, copy in jobs:
        pl.when(have)(copy.wait)


def unpack_b(gots):
    return pl.pallas_call(
        unpack_b_kernel,
        out_shape=jax.ShapeDtypeStruct((KZ * BS, CB * BS), F32),
        in_specs=[HBM] * NZ,
        out_specs=VMEM,
        scratch_shapes=[
            pltpu.SMEM((NZ, KZ * MET, BS), F32),
            pltpu.SemaphoreType.DMA((NZ, KZ * CAP)),
            pltpu.SemaphoreType.DMA((NZ,)),
        ],
        name="unpack_b",
    )(*gots)


def split(value):
    high = value.astype(jnp.bfloat16)
    return high, (value - high.astype(F32)).astype(jnp.bfloat16)


def k_order():
    _, y, x, c, step = place()
    ks = []
    for dy in range(NY):
        y_at = lax.rem(y + dy, NY)
        for dx in (0, -step, step, 2):
            for dc in range(NC):
                x_at = lax.rem(x + NX + (dx if dc == 0 or isinstance(dx, int) else -dx), NX)
                ks.append(y_at * (NX * NC) + x_at * NC + lax.rem(c + dc, NC))
    return ks


TM, TM_LAST = 512, 1024


def product_kernel(last, mask, *refs):
    refs = list(refs)
    b_pieces = [refs.pop(0) for _ in range(1 if last else NZ - 1)]
    pieces = [refs.pop(0) for _ in range(KB)]
    before = refs.pop(0) if last else None
    out, rows, panel, stack, a_sems, b_sems = refs
    tile, tiles = pl.program_id(0), pl.num_programs(0)
    tm = out.shape[0]
    depth = len(b_pieces) * KZ * BS
    z_now, step = place()[0], place()[4]

    def fetch(at, wait):
        buffer = lax.rem(at, 2)
        for piece, k in zip(pieces, k_order()):
            hop = lax.rem((z_now - lax.div(k, KZ)) * step + 2 * NZ, NZ)
            slot = lax.rem(k, KZ) + (0 if last else KZ * jnp.minimum(hop, 2))
            copy = pltpu.make_async_copy(
                piece.at[pl.ds(pl.multiple_of(at * tm, tm), tm)],
                rows.at[buffer, :, pl.ds(pl.multiple_of(slot * BS, BS), BS)],
                a_sems.at[buffer, slot],
            )
            pl.when(hop == 2 if last else hop != 2)(copy.wait if wait else copy.start)

    @pl.when(tile == 0)
    def _():
        jobs = [
            pltpu.make_async_copy(piece, panel.at[pl.ds(i * KZ * BS, KZ * BS)], b_sems.at[i])
            for i, piece in enumerate(b_pieces)
        ]
        for job in jobs:
            job.start()
        fetch(tile, False)
        fetch(tile + 1, False)
        for job in jobs:
            job.wait()
        high, low = split(panel[...])
        stack[pl.ds(0, depth), :] = high
        stack[pl.ds(depth, depth), :] = low

    fetch(tile, True)
    high, low = split(rows[lax.rem(tile, 2)])
    total = jnp.dot(
        jnp.concatenate([high, high], axis=1), stack[...], preferred_element_type=F32
    )
    total += jnp.dot(low, stack[pl.ds(0, depth), :], preferred_element_type=F32)
    if last:
        total += before[...]
        for r in range(tm // BS):
            for c in range(CB):
                keep = mask[tile * (tm // BS) + r, c].astype(F32)
                piece = total[r * BS : (r + 1) * BS, c * BS : (c + 1) * BS]
                out[pl.ds(r * BS, BS), pl.ds(c * BS, BS)] = piece * keep
    else:
        out[...] = total
    pl.when(tile + 2 < tiles)(lambda: fetch(tile + 2, False))


def product(mask, b_pieces, a_pieces, before=None):
    height, cols = RB * BS, CB * BS
    depth = len(b_pieces) * KZ * BS
    last = before is not None
    tm = TM_LAST if last else TM
    c_spec = pl.BlockSpec((tm, cols), lambda t: (t, 0))
    return pl.pallas_call(
        functools.partial(product_kernel, last),
        grid=(height // tm,),
        out_shape=jax.ShapeDtypeStruct((height, cols), F32),
        in_specs=[SMEM] + [HBM] * (len(b_pieces) + KB) + [c_spec] * last,
        out_specs=c_spec,
        scratch_shapes=[
            pltpu.VMEM((2, tm, depth), F32),
            pltpu.VMEM((depth, cols), F32),
            pltpu.VMEM((2 * depth, cols), jnp.bfloat16),
            pltpu.SemaphoreType.DMA((2, depth // BS)),
            pltpu.SemaphoreType.DMA((len(b_pieces),)),
        ],
        compiler_params=pltpu.CompilerParams(vmem_limit_bytes=58 << 20),
        cost_estimate=pl.CostEstimate(
            flops=6 * height * cols * depth,
            bytes_accessed=4 * (height * depth + depth * cols + 2 * height * cols),
            transcendentals=0,
        ),
        name="product",
    )(mask, *b_pieces, *a_pieces, *([before] if last else []))


def per_device(a_blocks, a_rows, a_cols, a_counts, b_blocks, b_rows, b_cols, b_counts, out_mask):
    a_send = pack_a(a_counts.reshape(-1), a_rows.reshape(-1), a_blocks.reshape(-1, BS, BS))
    a_got = lax.all_to_all(a_send, "col", split_axis=0, concat_axis=0, tiled=True)
    b_send = pack_b(
        after(b_counts.reshape(-1), a_send), b_cols.reshape(-1), b_blocks.reshape(-1, BS, BS)
    )
    b_got = [b_send[0]] + [row_shift(b_send[rel], dz=rel) for rel in range(1, NZ)]
    b_part = unpack_b(b_got)
    own = unpack_a(a_got)
    joined = lax.optimization_barrier

    def swap(value, *earlier):
        return col_shift(after(value, *earlier) if earlier else value, dc=1)

    def hop(value, step):
        return col_shift(value, dx=step, by_core=True)

    with jax.named_scope("t_F"):
        v_F = hop(own, 1)
    with jax.named_scope("t_S"):
        v_S = row_shift(b_part, dy=1)
    with jax.named_scope("t_G"):
        v_G = hop(own, -1)
    with jax.named_scope("t_H"):
        v_H = hop(after(v_F, v_G), 1)
    with jax.named_scope("t_cown"):
        v_cown = swap(after(own, v_G))
    with jax.named_scope("t_Y"):
        v_Y = col_shift(own, dy=1)
    with jax.named_scope("t_cF"):
        v_cF = swap(v_F)
    with jax.named_scope("t_cY"):
        v_cY = swap(after(v_Y, v_G))
    with jax.named_scope("t_cH"):
        v_cH = swap(v_H)
    with jax.named_scope("t_cG"):
        v_cG = swap(v_G)
    with jax.named_scope("t_YF"):
        v_YF = hop(after(v_Y, v_G), 1)
    with jax.named_scope("t_YG"):
        v_YG = hop(v_Y, -1)
    with jax.named_scope("t_cYF"):
        v_cYF = swap(after(v_YF, v_cown))
    with jax.named_scope("t_cYG"):
        v_cYG = swap(v_YG)
    v_b_here = b_part + after(v_S, v_F)
    with jax.named_scope("t_YH"):
        v_YH = hop(after(v_YF, v_YF), 1)
    with jax.named_scope("t_bG"):
        v_bG = row_shift_by_core(v_b_here, -1)
    with jax.named_scope("t_bF"):
        v_bF = row_shift_by_core(v_b_here, 1)
    with jax.named_scope("t_bH"):
        v_bH = row_shift_by_core(after(v_bF, v_G), 1)
    with jax.named_scope("t_cYH"):
        v_cYH = swap(v_YH)
    b_all = (v_b_here, v_bF, v_bG, v_bH)
    a_all = [own, v_cown, v_F, v_cF, v_G, v_cG, v_H, v_cH]
    a_all += [v_Y, v_cY, v_YF, v_cYF, v_YG, v_cYG, v_YH, v_cYH]
    total = product(out_mask, b_all[:3], a_all)
    return product(out_mask, b_all[3:], a_all, before=total)


def solution(mesh):
    lists = P("row", "col", None)
    blocks = P("row", "col", None, None, None)
    in_specs = (blocks, lists, lists, lists, blocks, lists, lists, lists, P("row", "col"))
    return jax.shard_map(
        per_device, mesh=mesh, in_specs=in_specs, out_specs=P("row", "col"), check_vma=False
    )
```
